32 devices in a mesh: seq: 4 (over x, core), chan: 8 (over z, y).
Axes of the slice: x: 2, y: 2, z: 4, core: 2. Of those that a mesh axis runs over, the one named last changes fastest.
Arguments:
- signal_in: bfloat16 [1024, 8192], P('seq', 'chan'), may hold values from -6 to 6
- gate_in: bfloat16 [1024, 8192], P('seq', 'chan'), may hold values from -6 to 6
- outer_gate: bfloat16 [1024, 8192], P('seq', 'chan'), may hold values from -6 to 6
- cotangent: bfloat16 [1024, 8192], P('seq', 'chan'), may hold values from -6 to 6
- residues: float32 [16, 512], replicated, may hold values from -4 to 4
- log_rates: float32 [16, 512], replicated, may hold values from -11 to -2.5
Outputs:
- grad_signal: bfloat16 [1024, 8192], P('seq', 'chan')
- grad_gate: bfloat16 [1024, 8192], P('seq', 'chan')
- grad_outer: bfloat16 [1024, 8192], P('seq', 'chan')
- grad_residues: float32 [16, 512], replicated
- grad_log_rates: float32 [16, 512], replicated
The draws below stay inside these ranges and needn't reach their ends.
All inputs are finite; a program needn't handle non-finite values.
Results may differ from the reference program's by a relative error of at most 0.01.
Values may be sent and summed in bfloat16 or wider, within the bound.
A program may use at most 64 MiB of HBM per device.

```python
import math
import jax
import jax.numpy as jnp
from jax import lax

D = 8192
FILTERS = 512
MODES = 16
TOKENS = 1024


def block_scale(key, dims, cuts, least, top_value):
    loudness = 1.0
    for position, blocks in cuts:
        steps = jax.random.uniform(jax.random.fold_in(jax.random.fold_in(key, 6), position), (blocks,), jnp.float32, least / len(cuts), top_value / len(cuts))
        loudness = loudness * jnp.repeat(jnp.exp(steps), dims[position] // blocks).reshape((-1,) + (1,) * (len(dims) - 1 - position))
    return loudness


def bell_draw(key, shape, deviation, reach, cuts=(), dtype=jnp.bfloat16):
    values = jax.random.normal(key, shape, jnp.float32) * deviation
    if len(cuts) > 0:
        values = block_scale(key, shape, cuts, -0.22, 0.18) * values
    return jnp.clip(values, min=-reach, max=reach).astype(dtype)


def setup_inputs(seed: int = 0) -> dict:
    arg_keys = jax.random.split(jax.random.key(seed), 7)
    signal_in = bell_draw(arg_keys[0], (TOKENS, D), 1.0, 6.0, ((0, 4), (1, 8)))
    gate_in = bell_draw(arg_keys[1], (TOKENS, D), 1.0, 6.0, ((0, 4), (1, 8)))
    outer_gate = bell_draw(arg_keys[2], (TOKENS, D), 1.0, 6.0, ((0, 4), (1, 8)))
    cotangent = bell_draw(arg_keys[3], (TOKENS, D), 1.0, 6.0, ((0, 4), (1, 8)))
    residues = bell_draw(arg_keys[4], (MODES, FILTERS), 0.6, 4.0, (), jnp.float32)
    log_rates = jnp.clip(jax.random.uniform(arg_keys[5], (MODES, FILTERS), jnp.float32, -11.0, -2.5), -11.0, -2.5)
    return dict(signal_in=signal_in, gate_in=gate_in, outer_gate=outer_gate, cotangent=cotangent, residues=residues, log_rates=log_rates)


def reference(signal_in, gate_in, outer_gate, cotangent, residues, log_rates):
    width = math.gcd(FILTERS, 256)
    count = D // width
    period = 2 * TOKENS
    scale = TOKENS ** -0.5
    norm = (TOKENS * D // FILTERS) ** -0.5
    times = jnp.arange(TOKENS).astype(jnp.float32)

    def columns(array, start):
        return lax.dynamic_slice_in_dim(array, start, width, 1).astype(jnp.float32)

    def one_block(carry, index):
        start = index * width
        offset = start % FILTERS
        signal = columns(signal_in, start)
        gate = columns(gate_in, start)
        outer = columns(outer_gate, start)
        upstream = columns(cotangent, start)
        residue_columns = lax.dynamic_slice_in_dim(residues, offset, width, 1)
        rate = jnp.exp(lax.dynamic_slice_in_dim(log_rates, offset, width, 1))
        basis = jnp.exp(-rate[None] * times[:, None, None])
        impulse = scale * jnp.sum(residue_columns[None] * basis, 1)
        gated = lax.optimization_barrier((signal * gate).astype(jnp.bfloat16)).astype(jnp.float32)
        weighted = lax.optimization_barrier((upstream * outer).astype(jnp.bfloat16)).astype(jnp.float32)
        spectrum_gated = jnp.fft.rfft(gated, n=period, axis=0)
        spectrum_weighted = jnp.fft.rfft(weighted, n=period, axis=0)
        spectrum_impulse = jnp.fft.rfft(impulse, n=period, axis=0)
        convolved = jnp.fft.irfft(spectrum_gated * spectrum_impulse, n=period, axis=0)[:TOKENS]
        grad_gated = jnp.fft.irfft(spectrum_weighted * jnp.conj(spectrum_impulse), n=period, axis=0)[:TOKENS]
        lag_grad = jnp.fft.irfft(spectrum_weighted * jnp.conj(spectrum_gated), n=period, axis=0)[:TOKENS]
        moment = lag_grad[:, None, :] * basis
        first = scale * jnp.sum(moment, 0)
        second = -scale * residue_columns * rate * jnp.sum(moment * times[:, None, None], 0)
        total_first = lax.dynamic_update_slice_in_dim(carry[0], lax.dynamic_slice_in_dim(carry[0], offset, width, 1) + first, offset, 1)
        total_second = lax.dynamic_update_slice_in_dim(carry[1], lax.dynamic_slice_in_dim(carry[1], offset, width, 1) + second, offset, 1)
        outputs = ((grad_gated * gate).astype(jnp.bfloat16), (grad_gated * signal).astype(jnp.bfloat16), (upstream * convolved).astype(jnp.bfloat16))
        return (total_first, total_second), outputs

    zeros = jnp.zeros((MODES, FILTERS), jnp.float32)
    totals, pieces = lax.scan(one_block, (zeros, zeros), jnp.arange(count).astype(jnp.int32))

    def unblock(stacked):
        return jnp.transpose(stacked, (1, 0, 2)).reshape(TOKENS, D)

    return unblock(pieces[0]), unblock(pieces[1]), unblock(pieces[2]), norm * totals[0], norm * totals[1]
```

```python
import functools
import math

import jax
import jax.numpy as jnp
from jax import lax
from jax.experimental import pallas as pl
from jax.experimental.pallas import tpu as pltpu
from jax.sharding import PartitionSpec as P

LANES = 128
SUB = 8
SEG = 16
f32 = jnp.float32
MESH = pl.DeviceIdType.MESH


def rows_of(ref, first, stride):
    return ref[pl.ds(first, SUB, stride=stride), :]


def spread(ref, row):
    return jnp.broadcast_to(ref[pl.ds(row, 1), :], (SUB, LANES))


def filter_lanes(block, cols, filters):
    start = lax.axis_index("chan") * cols + block * LANES
    return pl.ds(pl.multiple_of(lax.rem(start, filters), LANES), LANES)


def block_lanes(block):
    return pl.ds(pl.multiple_of(block * LANES, LANES), LANES)


def tree(values):
    while len(values) > 1:
        values = [values[i] + values[i + 1] for i in range(0, len(values), 2)]
    return values[0]


def state_block(scale, block, fl, sig, gate, outer, cot, res, logr, g_s, w_s, a_s, h_s, pw_s, st, lag_s, xs, ys, edge,
                moment, gsum):
    rows = sig.shape[0]
    modes = res.shape[0]
    segs = rows // SEG
    groups = segs // SUB
    g_s[...] = (sig[...].astype(f32) * gate[...].astype(f32)).astype(jnp.bfloat16).astype(f32)
    w_s[...] = (cot[...].astype(f32) * outer[...].astype(f32)).astype(jnp.bfloat16).astype(f32)
    rate = jnp.exp(logr[:, fl])
    amp = res[:, fl] * scale
    a = jnp.exp(-rate)
    a_s[...] = a
    power = jnp.ones((modes, LANES), f32)
    for u in range(SEG):
        pw_s[u * modes : (u + 1) * modes, :] = power
        h_s[u : u + 1, :] = jnp.sum(amp * power, 0, keepdims=True)
        power = power * a
    seg_decay = power

    @pl.loop(0, groups)
    def _(group):
        base = group * (SUB * SEG)
        for half in range(0, modes, SUB):
            decay = [spread(a_s, half + k) for k in range(SUB)]
            zero = jnp.zeros((SUB, LANES), f32)
            x, z, y, v = ([zero] * SUB for _ in range(4))
            for j in range(SEG):
                gj = rows_of(g_s, base + j, SEG)
                wj = rows_of(w_s, base + SEG - 1 - j, SEG)
                for k in range(SUB):
                    x[k] = decay[k] * (x[k] + gj)
                    z[k] = decay[k] * z[k] + x[k]
                    t = decay[k] * y[k]
                    y[k] = t + wj
                    v[k] = decay[k] * v[k] + t
            for k in range(SUB):
                at = pl.ds(pl.multiple_of((half + k) * segs + group * SUB, SUB), SUB)
                st[0, at, :] = x[k]
                st[1, at, :] = z[k]
                st[2, at, :] = y[k]
                st[3, at, :] = v[k]
        g = [rows_of(g_s, base + j, SEG) for j in range(SEG)]
        w = [rows_of(w_s, base + j, SEG) for j in range(SEG)]
        for u in range(SEG):
            total = w[u] * g[0]
            for j in range(u + 1, SEG):
                total = total + w[j] * g[j - u]
            lag_s[pl.ds(pl.multiple_of((group * SEG + u) * SUB, SUB), SUB), :] = total

    gr = jnp.zeros((modes, LANES), f32)
    gl = jnp.zeros((modes, LANES), f32)
    for u in range(SEG):
        total = lag_s[u * SUB : (u + 1) * SUB, :]
        for group in range(1, groups):
            first = (group * SEG + u) * SUB
            total = total + lag_s[first : first + SUB, :]
        term = jnp.sum(total, 0, keepdims=True) * pw_s[u * modes : (u + 1) * modes, :]
        gr = gr + term
        if u > 0:
            gl = gl + float(u) * term
    x = jnp.zeros((modes, LANES), f32)
    xd = x
    for seg in range(segs):
        at = pl.ds(seg, modes, stride=segs)
        e, d, y, v = (st[i, at, :] for i in range(4))
        xs[seg * modes : (seg + 1) * modes, :] = x
        if seg > 0:
            gr = gr + x * y
            gl = gl + (xd * y + x * v)
        xd = seg_decay * (xd + float(SEG) * x) + d
        x = seg_decay * x + e
    y = jnp.zeros((modes, LANES), f32)
    yv = y
    for seg in reversed(range(segs)):
        at = pl.ds(seg, modes, stride=segs)
        ys[seg * modes : (seg + 1) * modes, :] = y
        yv = st[3, at, :] + seg_decay * (yv + float(SEG) * y)
        y = st[2, at, :] + seg_decay * y
    edge[0, block] = x
    edge[1, block] = y
    moment[0] = xd
    moment[1] = yv
    gsum[0] = gr
    gsum[1] = gl


def inner_block(rows, g_s, w_s, h_s, conv, grad):
    @pl.loop(0, rows // (SEG * SUB))
    def _(group):
        base = group * (SUB * SEG)
        h = [spread(h_s, u) for u in range(SEG)]
        g = [rows_of(g_s, base + j, SEG) for j in range(SEG)]
        for j in range(SEG):
            forward = h[0] * g[j]
            for u in range(1, j + 1):
                forward = forward + h[u] * g[j - u]
            conv[pl.ds(base + j, SUB, stride=SEG), :] = forward
        w = [rows_of(w_s, base + j, SEG) for j in range(SEG)]
        for j in range(SEG):
            backward = h[0] * w[j]
            for u in range(1, SEG - j):
                backward = backward + h[u] * w[j + u]
            grad[pl.ds(base + j, SUB, stride=SEG), :] = backward


def gradient_block(scale, parts, span, block, fl, edges, edge, moment, gsum, res, logr, totals, carry):
    place = lax.axis_index("seq")
    rate = jnp.exp(logr[:, fl])
    x0 = jnp.zeros(rate.shape, f32)
    xm = x0
    y0 = x0
    for other in range(parts):
        ahead = jnp.maximum(place - 1 - other, 0).astype(f32) * float(span)
        behind = jnp.maximum(other - place - 1, 0).astype(f32) * float(span)
        value = edges[other, block]
        e = jnp.where(other < place, value, 0.0) * jnp.exp(-rate * ahead)
        x0 = x0 + e
        xm = xm + ahead * e
        y0 = y0 + jnp.where(other > place, value, 0.0) * jnp.exp(-rate * behind)
    carry[0] = x0
    carry[1] = y0
    w = edge[1, block]
    gr = gsum[0] + x0 * w
    gl = gsum[1] + x0 * moment[1] + xm * w + moment[0] * y0
    totals[0, :, fl] = totals[0, :, fl] + scale * gr
    totals[1, :, fl] = totals[1, :, fl] - scale * (res[:, fl] * rate) * gl


def output_block(scale, fl, res, logr, conv, grad, xs, ys, carry, a_s, p_s, q_s):
    rows = conv.shape[0]
    modes = res.shape[0]
    segs = rows // SEG
    rate = jnp.exp(logr[:, fl])
    amp = res[:, fl] * scale
    a_s[...] = jnp.exp(-rate)
    seg_decay = jnp.exp(-rate * float(SEG))
    p = amp * carry[0]
    q = amp * carry[1]
    for seg in range(segs):
        at = slice(seg * modes, (seg + 1) * modes)
        p_s[at, :] = amp * xs[at, :] + p
        p = p * seg_decay
        back = segs - 1 - seg
        at = slice(back * modes, (back + 1) * modes)
        q_s[at, :] = amp * ys[at, :] + q
        q = q * seg_decay

    @pl.loop(0, segs // SUB)
    def _(group):
        base = group * (SUB * SEG)
        for half in range(0, modes, SUB):
            decay = [spread(a_s, half + k) for k in range(SUB)]
            p = [rows_of(p_s, group * (SUB * modes) + half + k, modes) for k in range(SUB)]
            q = [rows_of(q_s, group * (SUB * modes) + half + k, modes) for k in range(SUB)]
            for j in range(SEG):
                at = pl.ds(base + j, SUB, stride=SEG)
                conv[at, :] = conv[at, :] + tree(p)
                q = [decay[k] * q[k] for k in range(SUB)]
                at = pl.ds(base + SEG - 1 - j, SUB, stride=SEG)
                grad[at, :] = grad[at, :] + tree(q)
                if j < SEG - 1:
                    p = [decay[k] * p[k] for k in range(SUB)]


def whole_kernel(
    scale, norm, parts, groups_chan,
    sig_h, gate_h, outer_h, cot_h, res_h, logr_h,
    out_sig_h, out_gate_h, out_outer_h, sums_h,
    ins, params, outs, g_s, w_s, conv, grad, xs, ys, edge, edges, moment, gsum, carry, h_s,
    a_s, pw_s, st, lag_s, p_s, q_s, totals, pieces, landed, slots, final,
    in_sem, param_sem, out_sem, edge_send, edge_recv, rs_send, rs_recv, mid_send, mid_recv, end_send, end_recv,
):
    rows, cols = sig_h.shape
    modes, filters = res_h.shape
    blocks = cols // LANES
    place = lax.axis_index("seq")
    column = lax.axis_index("chan")
    pairs = pair_size(groups_chan)
    barrier = pltpu.get_barrier_semaphore()

    def remote(src, dst, send, recv, device):
        return pltpu.make_async_remote_copy(
            src_ref=src, dst_ref=dst, send_sem=send, recv_sem=recv, device_id=device, device_id_type=MESH
        )

    low = lax.rem(column, pairs)
    high = column // pairs
    upper = groups_chan // pairs
    team = parts * pairs
    member = place * pairs + low

    def mate(index):
        return {"seq": index // pairs, "chan": high * pairs + lax.rem(index, pairs)}

    def tower(index):
        return {"chan": index * pairs + low}

    for d in range(1, team):
        pl.semaphore_signal(barrier, inc=1, device_id=mate(lax.rem(member + d, team)), device_id_type=MESH)
    for d in range(1, upper):
        pl.semaphore_signal(barrier, inc=1, device_id=tower(lax.rem(high + d, upper)), device_id_type=MESH)

    param_copies = [
        pltpu.make_async_copy(ref, params.at[i], param_sem.at[i]) for i, ref in enumerate((res_h, logr_h))
    ]
    for copy in param_copies:
        copy.start()

    def fetch(i, ref, block):
        return pltpu.make_async_copy(ref.at[:, block_lanes(block)], ins.at[i, block], in_sem.at[i, block])

    whole_inputs = (sig_h, gate_h, outer_h, cot_h)

    @pl.loop(0, blocks)
    def _(block):
        for i, ref in enumerate(whole_inputs):
            fetch(i, ref, block).start()

    for copy in param_copies:
        copy.wait()
    pl.semaphore_wait(barrier, team - 1 + upper - 1)
    res, logr = params.at[0], params.at[1]

    def edge_copy(d, block):
        other = lax.rem(place + d, parts)
        which = jnp.where(other > place, 0, 1)
        if block is None:
            src, dst = edge.at[which], edges.at[place]
        else:
            src, dst = edge.at[which, block], edges.at[place, block]
        return remote(src, dst, edge_send.at[d], edge_recv.at[d], {"seq": other})

    @pl.loop(0, blocks)
    def _(block):
        for i, ref in enumerate(whole_inputs):
            fetch(i, ref, block).wait()
        sig, gate, outer, cot = (ins.at[i, block] for i in range(4))
        state_block(
            scale, block, filter_lanes(block, cols, filters), sig, gate, outer, cot, res, logr,
            g_s.at[block], w_s.at[block], a_s, h_s.at[block], pw_s, st, lag_s, xs.at[block], ys.at[block], edge,
            moment.at[block], gsum.at[block],
        )
        for d in range(1, parts):
            edge_copy(d, block).start()

    def inner(first, last):
        @pl.loop(first, last)
        def _(block):
            inner_block(rows, g_s.at[block], w_s.at[block], h_s.at[block], conv.at[block], grad.at[block])

    early = (blocks + 1) // 2
    inner(0, early)
    for d in range(1, parts):
        source = lax.rem(place + parts - d, parts)
        remote(edge.at[0], edges.at[source], edge_send.at[d], edge_recv.at[d], {"seq": source}).wait_recv()
    totals[...] = jnp.zeros_like(totals)
    edges[place] = jnp.zeros_like(edge[0])

    @pl.loop(0, blocks)
    def _(block):
        gradient_block(
            scale, parts, rows, block, filter_lanes(block, cols, filters), edges, edge, moment.at[block],
            gsum.at[block], res, logr, totals, carry.at[block],
        )

    size = 2 * modes // team
    for p in range(team):
        which, first = divmod(p * size, modes)
        pieces[p] = totals[which, first : first + size, :]

    def scatter(d):
        other = lax.rem(member + d, team)
        return remote(pieces.at[other], landed.at[d], rs_send.at[d], rs_recv.at[d], mate(other))

    def middle(d, back=False):
        other = lax.rem(high + (upper - d if back else d), upper)
        slot = slots.at[other if back else high]
        return remote(slot, slot, mid_send.at[d], mid_recv.at[d], tower(other))

    def ending(d, back=False):
        other = lax.rem(member + (team - d if back else d), team)
        slot = final.at[other if back else member]
        return remote(slot, slot, end_send.at[d], end_recv.at[d], mate(other))

    for d in range(1, team):
        scatter(d).start()
    inner(early, blocks)

    def put(i, block):
        target = (out_sig_h, out_gate_h, out_outer_h)[i]
        return pltpu.make_async_copy(outs.at[i, block], target.at[:, block_lanes(block)], out_sem.at[i, block])

    def outputs(first, last):
        if first == last:
            return

        @pl.loop(first, last)
        def _(block):
            output_block(
                scale, filter_lanes(block, cols, filters), res, logr, conv.at[block], grad.at[block], xs.at[block],
                ys.at[block], carry.at[block], a_s, p_s, q_s,
            )
            d = grad[block]
            at = block_lanes(block)
            out_sig_h[:, at] = (d * ins[1, block].astype(f32)).astype(jnp.bfloat16)
            out_gate_h[:, at] = (d * ins[0, block].astype(f32)).astype(jnp.bfloat16)
            out_outer_h[:, at] = (conv[block] * ins[3, block].astype(f32)).astype(jnp.bfloat16)

    first_stop = blocks // 8
    second_stop = blocks - blocks // 4
    outputs(0, first_stop)
    for d in range(1, team):
        scatter(d).wait_recv()
    mine = pieces[member]
    for d in range(1, team):
        mine = mine + landed[d]
    slots[high] = mine
    for d in range(1, upper):
        middle(d).start()
    outputs(first_stop, second_stop)
    for d in range(1, upper):
        middle(d, back=True).wait_recv()
    summed = slots[0]
    for other in range(1, upper):
        summed = summed + slots[other]
    final[member] = norm * summed
    for d in range(1, team):
        ending(d).start()
    outputs(second_stop, blocks)
    for d in range(1, team):
        ending(d, back=True).wait_recv()
    for p in range(team):
        which, first = divmod(p * size, modes)
        sums_h[which, first : first + size, :] = final[p]

    for d in range(1, parts):
        edge_copy(d, None).wait_send()
    for d in range(1, team):
        scatter(d).wait_send()
        ending(d).wait_send()
    for d in range(1, upper):
        middle(d).wait_send()


def pass_kernel(sig, gate, outer, sums, out_sig, out_gate, out_outer, out_res, out_rate, sem):
    pairs = ((sig, out_sig), (gate, out_gate), (outer, out_outer), (sums.at[0], out_res), (sums.at[1], out_rate))
    copies = [pltpu.make_async_copy(src, dst, sem.at[n]) for n, (src, dst) in enumerate(pairs)]
    for copy in copies:
        copy.start()
    for copy in copies:
        copy.wait()


def pair_size(columns):
    return 2 if columns % 2 == 0 else 1


def on_device(signal_in, gate_in, outer_gate, cotangent, residues, log_rates):
    parts = lax.axis_size("seq")
    groups_chan = lax.axis_size("chan")
    rows, cols = signal_in.shape
    modes, filters = residues.shape
    total = parts * rows
    blocks = cols // LANES
    segs = rows // SEG
    groups = segs // SUB
    pairs = pair_size(groups_chan)
    team = parts * pairs
    upper = groups_chan // pairs
    size = 2 * modes // team
    scale = float(total) ** (-0.5)
    norm = float(total * cols * groups_chan // filters) ** (-0.5)
    whole = pl.BlockSpec(memory_space=pltpu.VMEM)
    far = pl.BlockSpec(memory_space=pl.ANY)
    shape = jax.ShapeDtypeStruct
    small = pltpu.VMEM((modes, LANES), f32)
    tiles = pltpu.VMEM((blocks, rows, LANES), f32)
    states = pltpu.VMEM((blocks, segs * modes, LANES), f32)
    pair = pltpu.VMEM((blocks, 2, modes, LANES), f32)
    dma = pltpu.SemaphoreType.DMA
    narrow = shape((rows, cols), jnp.bfloat16)
    *products, sums = pl.pallas_call(
        functools.partial(whole_kernel, scale, norm, parts, groups_chan),
        out_shape=(
            pltpu.VMEM((rows, cols), jnp.bfloat16),
            pltpu.VMEM((rows, cols), jnp.bfloat16),
            pltpu.VMEM((rows, cols), jnp.bfloat16),
            pltpu.VMEM((2, modes, filters), f32),
        ),
        in_specs=[pl.BlockSpec(memory_space=pltpu.HBM)] * 6,
        out_specs=(whole,) * 4,
        scratch_shapes=[
            pltpu.VMEM((4, blocks, rows, LANES), jnp.bfloat16),
            pltpu.VMEM((2, modes, filters), f32),
            pltpu.VMEM((3, blocks, rows, LANES), jnp.bfloat16),
            tiles,
            tiles,
            tiles,
            tiles,
            states,
            states,
            pltpu.VMEM((2, blocks, modes, LANES), f32),
            pltpu.VMEM((parts, blocks, modes, LANES), f32),
            pair,
            pair,
            pair,
            pltpu.VMEM((blocks, SEG, LANES), f32),
            small,
            pltpu.VMEM((SEG * modes, LANES), f32),
            pltpu.VMEM((4, modes * segs, LANES), f32),
            pltpu.VMEM((groups * SEG * SUB, LANES), f32),
            pltpu.VMEM((segs * modes, LANES), f32),
            pltpu.VMEM((segs * modes, LANES), f32),
            pltpu.VMEM((2, modes, filters), f32),
            pltpu.VMEM((team, size, filters), f32),
            pltpu.VMEM((team, size, filters), f32),
            pltpu.VMEM((upper, size, filters), f32),
            pltpu.VMEM((team, size, filters), f32),
            dma((4, blocks)),
            dma((2,)),
            dma((3, blocks)),
            dma((parts,)),
            dma((parts,)),
            dma((team,)),
            dma((team,)),
            dma((upper,)),
            dma((upper,)),
            dma((team,)),
            dma((team,)),
        ],
        compiler_params=pltpu.CompilerParams(
            collective_id=0, has_side_effects=True
        ),
        name="whole",
    )(signal_in, gate_in, outer_gate, cotangent, residues, log_rates)
    return pl.pallas_call(
        pass_kernel,
        out_shape=(narrow, narrow, narrow, shape((modes, filters), f32), shape((modes, filters), f32)),
        in_specs=[whole] * 4,
        out_specs=(far,) * 5,
        scratch_shapes=[dma((5,))],
        name="passed",
    )(*(pltpu.with_memory_space_constraint(a, pltpu.VMEM) for a in (*products, sums)))


def solution(mesh):
    placed = (P("seq", "chan"), P("seq", "chan"), P("seq", "chan"), P("seq", "chan"), P(), P())
    return jax.shard_map(
        on_device,
        mesh=mesh,
        in_specs=placed,
        out_specs=(P("seq", "chan"), P("seq", "chan"), P("seq", "chan"), P(), P()),
        check_vma=False,
    )
```

```python
import functools
import math

import jax
import jax.numpy as jnp
from jax import lax
from jax.experimental import pallas as pl
from jax.experimental.pallas import tpu as pltpu
from jax.sharding import PartitionSpec as P

LANES = 128
SUB = 8
SEG = 16
PACK = 16
f32 = jnp.float32
bf16 = jnp.bfloat16
MESH = pl.DeviceIdType.MESH


def rows_of(ref, first, stride):
    return ref[pl.ds(first, SUB, stride=stride), :]


def spread(ref, row):
    return jnp.broadcast_to(ref[pl.ds(row, 1), :], (SUB, LANES))


def spread_narrow(ref, row):
    return jnp.broadcast_to(ref[pl.ds(row, 1), :], (PACK, LANES)).astype(bf16)


def block_lanes(block):
    return pl.ds(pl.multiple_of(block * LANES, LANES), LANES)


def filter_lanes(block, cols, filters):
    start = lax.axis_index("chan") * cols + block * LANES
    return pl.ds(pl.multiple_of(lax.rem(start, filters), LANES), LANES)


def tree(values):
    while len(values) > 1:
        paired = [values[i] + values[i + 1] for i in range(0, len(values) - 1, 2)]
        values = paired + values[len(paired) * 2 :]
    return values[0]


def moments(terms, last):
    quads, weighted = [], []
    for first in range(0, len(terms), 4):
        p = [terms[first]]
        for term in terms[first + 1 : first + 4]:
            p.append(p[-1] + term)
        quads.append(p[3])
        weighted.append(tree(p if last else p[:3]))
    q = [quads[0]]
    for quad in quads[1:]:
        q.append(q[-1] + quad)
    return q[-1], tree(weighted) + 4.0 * tree(q[:-1])


def state_block(scale, place, fb, local, fl, ins, res, logr, g_s, w_s, gt, wt, h_s, pw_s, st, lag_s, xs, ys, edges):
    rows = g_s.shape[1]
    modes = res.shape[0]
    segs = rows // SEG
    reps = g_s.shape[0] // local
    rate = jnp.exp(logr[:, fl])
    amp = res[:, fl] * scale
    a = jnp.exp(-rate)
    power = jnp.ones((modes, LANES), f32)
    for u in range(SEG + 1):
        pw_s[u * modes : (u + 1) * modes, :] = power
        if u < SEG:
            h_s[fb, u : u + 1, :] = jnp.sum(amp * power, 0, keepdims=True)
            power = power * a
    seg_decay = power

    for rep in range(reps):
        block = rep * local + fb
        sig, gate, outer, cot = (ins[i, block].astype(f32) for i in range(4))
        g_s[block] = (sig * gate).astype(bf16).astype(f32)
        w_s[block] = (cot * outer).astype(bf16).astype(f32)
        for src, dst in ((g_s.at[block], gt), (w_s.at[block], wt)):
            for part in range(segs // PACK):
                base = part * PACK * SEG
                for j in range(SEG):
                    halves = [rows_of(src, base + half * SUB * SEG + j, SEG) for half in range(PACK // SUB)]
                    dst[rep, part, j * PACK : (j + 1) * PACK, :] = jnp.concatenate(halves, 0).astype(bf16)

    def phase(ref, rep, part, j):
        return ref[rep, part, j * PACK : (j + 1) * PACK, :]

    for k in range(modes):
        powers = [spread_narrow(pw_s, e * modes + k) for e in range(SEG + 1)]
        for rep in range(reps):
            for part in range(segs // PACK):
                x, d = moments([powers[SEG - j] * phase(gt, rep, part, j) for j in range(SEG)], True)
                back = [powers[j] * phase(wt, rep, part, j) for j in range(SEG - 1, 0, -1)]
                y, v = moments(back + [phase(wt, rep, part, 0)], False)
                at = slice(k * segs + part * PACK, k * segs + (part + 1) * PACK)
                for i, value in enumerate((x, d, y, v)):
                    st[rep, i, at, :] = value.astype(f32)

    lags = [None] * SEG
    for rep in range(reps):
        for part in range(segs // PACK):
            g = [phase(gt, rep, part, j) for j in range(SEG)]
            w = [phase(wt, rep, part, j) for j in range(SEG)]
            for u in range(SEG):
                total = tree([w[j] * g[j - u] for j in range(u, SEG)]).astype(f32)
                total = total[:SUB] + total[SUB:]
                if rep + part == 0:
                    lag_s[u * SUB : (u + 1) * SUB, :] = total
                else:
                    lag_s[u * SUB : (u + 1) * SUB, :] += total

    gr = jnp.zeros((modes, LANES), f32)
    gl = jnp.zeros((modes, LANES), f32)
    for u in range(SEG):
        total = jnp.sum(lag_s[u * SUB : (u + 1) * SUB, :], 0, keepdims=True)
        term = total * pw_s[u * modes : (u + 1) * modes, :]
        gr = gr + term
        if u > 0:
            gl = gl + float(u) * term
    zero = jnp.zeros((modes, LANES), f32)
    for rep in range(reps):
        block = rep * local + fb
        x, xd = zero, zero
        for seg in range(segs):
            at = pl.ds(seg, modes, stride=segs)
            e, d, y, v = (st[rep, i, at, :] for i in range(4))
            xs[block, seg * modes : (seg + 1) * modes, :] = x
            if seg > 0:
                gr = gr + x * y
                gl = gl + (xd * y + x * v)
            xd = seg_decay * (xd + float(SEG) * x) + d
            x = seg_decay * x + e
        y, yv = zero, zero
        for seg in reversed(range(segs)):
            at = pl.ds(seg, modes, stride=segs)
            ys[block, seg * modes : (seg + 1) * modes, :] = y
            yv = st[rep, 3, at, :] + seg_decay * (yv + float(SEG) * y)
            y = st[rep, 2, at, :] + seg_decay * y
        for i, value in enumerate((x, y, xd, yv)):
            edges[place, fb, i * reps + rep] = value.astype(bf16)
    edges[place, fb, 4 * reps] = gr.astype(bf16)
    edges[place, fb, 4 * reps + 1] = gl.astype(bf16)


def inner_block(rows, g_s, w_s, h_s, conv, grad):
    @pl.loop(0, rows // (SEG * SUB))
    def _(group):
        base = group * (SUB * SEG)
        h = [spread(h_s, u) for u in range(SEG)]
        g = [rows_of(g_s, base + j, SEG) for j in range(SEG)]
        for j in range(SEG):
            forward = h[0] * g[j]
            for u in range(1, j + 1):
                forward = forward + h[u] * g[j - u]
            conv[pl.ds(base + j, SUB, stride=SEG), :] = forward
        w = [rows_of(w_s, base + j, SEG) for j in range(SEG)]
        for j in range(SEG):
            backward = h[0] * w[j]
            for u in range(1, SEG - j):
                backward = backward + h[u] * w[j + u]
            grad[pl.ds(base + j, SUB, stride=SEG), :] = backward


def gradient_block(scale, span, fb, fl, edges, res, logr):
    parts = edges.shape[0]
    reps = edges.shape[2] // 4
    rate = jnp.exp(logr[:, fl])
    decay = jnp.exp(-rate * float(span))

    def value(source, i):
        return edges[source, fb, i].astype(f32)

    gr = tree([value(source, 4 * reps) for source in range(parts)])
    gl = tree([value(source, 4 * reps + 1) for source in range(parts)])
    for rep in range(reps):
        x = value(0, rep)
        xd = value(0, 2 * reps + rep)
        for source in range(1, parts):
            y = value(source, reps + rep)
            gr = gr + x * y
            gl = gl + (x * value(source, 3 * reps + rep) + xd * y)
            if source < parts - 1:
                xd = (xd + float(span) * x) * decay + value(source, 2 * reps + rep)
                x = x * decay + value(source, rep)
    return scale * gr, -scale * (res[:, fl] * rate) * gl


def carry_block(span, fb, rep, fl, edges, logr, carry):
    place = lax.axis_index("seq")
    parts = edges.shape[0]
    reps = edges.shape[2] // 4
    decay = jnp.exp(-jnp.exp(logr[:, fl]) * float(span))
    values = []
    for source in range(parts):
        which = jnp.where(source > place, reps, 0)
        values.append(edges[source, fb, which + rep].astype(f32))
    x = jnp.zeros(decay.shape, f32)
    y = x
    for source in range(parts):
        x = jnp.where(source < place, x * decay + values[source], x)
        back = parts - 1 - source
        y = jnp.where(back > place, y * decay + values[back], y)
    carry[0] = x
    carry[1] = y


def output_block(scale, fl, res, logr, conv, grad, xs, ys, carry, a_s, p_s, q_s):
    rows = conv.shape[0]
    modes = res.shape[0]
    segs = rows // SEG
    rate = jnp.exp(logr[:, fl])
    amp = res[:, fl] * scale
    a_s[...] = jnp.exp(-rate)
    seg_decay = jnp.exp(-rate * float(SEG))
    p = amp * carry[0]
    q = amp * carry[1]
    for seg in range(segs):
        at = slice(seg * modes, (seg + 1) * modes)
        p_s[at, :] = amp * xs[at, :] + p
        p = p * seg_decay
        back = segs - 1 - seg
        at = slice(back * modes, (back + 1) * modes)
        q_s[at, :] = amp * ys[at, :] + q
        q = q * seg_decay

    @pl.loop(0, segs // SUB)
    def _(group):
        base = group * (SUB * SEG)
        for half in range(0, modes, SUB):
            decay = [spread(a_s, half + k) for k in range(SUB)]
            p = [rows_of(p_s, group * (SUB * modes) + half + k, modes) for k in range(SUB)]
            q = [rows_of(q_s, group * (SUB * modes) + half + k, modes) for k in range(SUB)]
            for j in range(SEG):
                at = pl.ds(base + j, SUB, stride=SEG)
                conv[at, :] = conv[at, :] + tree(p)
                q = [decay[k] * q[k] for k in range(SUB)]
                at = pl.ds(base + SEG - 1 - j, SUB, stride=SEG)
                grad[at, :] = grad[at, :] + tree(q)
                if j < SEG - 1:
                    p = [decay[k] * p[k] for k in range(SUB)]


def whole_kernel(
    scale, norm, parts, groups_chan, owners,
    sig_h, gate_h, outer_h, cot_h, res_h, logr_h,
    out_sig, out_gate, out_outer, sums,
    ins, params, g_s, w_s, conv, grad, xs, ys, edges, carry, h_s, gt, wt,
    a_s, pw_s, st, lag_s, p_s, q_s, slots, final,
    in_sem, param_sem, edge_send, edge_recv, mid_send, mid_recv, end_send, end_recv,
):
    rows, cols = sig_h.shape
    modes, filters = res_h.shape
    blocks = cols // LANES
    local = edges.shape[1]
    reps = blocks // local
    per = local // owners
    kinds = final.shape[1]
    place = lax.axis_index("seq")
    column = lax.axis_index("chan")
    own = lax.rem(place, owners)
    cell = place - own
    barrier = pltpu.get_barrier_semaphore()

    def each(first, last, fn):
        if last - first <= 8:
            for d in range(first, last):
                fn(d)
        else:
            pl.loop(first, last)(fn)

    def remote(src, dst, send, recv, device):
        return pltpu.make_async_remote_copy(
            src_ref=src, dst_ref=dst, send_sem=send, recv_sem=recv, device_id=device, device_id_type=MESH
        )

    def greet(axis, index, size):
        def signal(d):
            other = lax.rem(index + d, size)
            pl.semaphore_signal(barrier, inc=1, device_id={axis: other}, device_id_type=MESH)

        each(1, size, signal)

    greet("chan", column, groups_chan)
    greet("seq", place, parts)

    param_copies = [
        pltpu.make_async_copy(ref, params.at[i], param_sem.at[i]) for i, ref in enumerate((res_h, logr_h))
    ]
    for copy in param_copies:
        copy.start()

    def fetch(i, ref, block):
        return pltpu.make_async_copy(ref.at[:, block_lanes(block)], ins.at[i, block], in_sem.at[i, block])

    whole_inputs = (sig_h, gate_h, outer_h, cot_h)

    def turn(i):
        return lax.rem(own * per + per + i, local)

    @pl.loop(0, local)
    def _(i):
        for rep in range(reps):
            for n, ref in enumerate(whole_inputs):
                fetch(n, ref, rep * local + turn(i)).start()

    for copy in param_copies:
        copy.wait()
    res, logr = params.at[0], params.at[1]

    def piece_copy(sender, fb, d, device):
        ref = edges.at[sender, fb]
        return remote(ref, ref, edge_send.at[d, fb], edge_recv.at[d, fb], device)

    def edge_copy(sender, receiver, fb, d, device):
        first = jnp.where(receiver > sender, 0, reps)
        ref = edges.at[sender, fb, pl.ds(first, reps)]
        return remote(ref, ref, edge_send.at[d, fb], edge_recv.at[d, fb], device)

    @pl.loop(0, local)
    def _(i):
        fb = turn(i)
        for rep in range(reps):
            for n, ref in enumerate(whole_inputs):
                fetch(n, ref, rep * local + fb).wait()
        state_block(
            scale, place, fb, local, filter_lanes(fb, cols, filters), ins, res, logr, g_s, w_s, gt, wt, h_s, pw_s, st,
            lag_s, xs, ys, edges,
        )

        @pl.when(i == 0)
        def _():
            pl.semaphore_wait(barrier, parts - 1 + groups_chan - 1)

        def send(d):
            other = lax.rem(place + d, parts)
            whose = lax.rem(other, owners)
            is_piece = jnp.logical_and(fb >= whose * per, fb < (whose + 1) * per)

            @pl.when(is_piece)
            def _():
                piece_copy(place, fb, d, {"seq": other}).start()

            @pl.when(jnp.logical_not(is_piece))
            def _():
                edge_copy(place, other, fb, d, {"seq": other}).start()

        each(1, parts, send)

    def inner(first, last):
        if first == last:
            return

        @pl.loop(first, last)
        def _(block):
            fb = lax.rem(block, local)
            inner_block(rows, g_s.at[block], w_s.at[block], h_s.at[fb], conv.at[block], grad.at[block])

    half = blocks // 2
    inner(0, half)

    def piece_arrived(d):
        source = lax.rem(place + parts - d, parts)
        for i in range(per):
            piece_copy(source, own * per + i, d, {"seq": source}).wait_recv()

    each(1, parts, piece_arrived)
    for i in range(per):
        fb = own * per + i
        first, second = gradient_block(scale, rows, fb, filter_lanes(fb, cols, filters), edges, res, logr)
        slots[column, i, 0] = first.astype(bf16)
        slots[column, i, 1] = second.astype(bf16)

    def middle(d, back=False):
        other = lax.rem(column + (groups_chan - d if back else d), groups_chan)
        slot = slots.at[other if back else column]
        return remote(slot, slot, mid_send.at[d], mid_recv.at[d], {"chan": other})

    def ending(d, back=False):
        other = lax.rem(own + (owners - d if back else d), owners)
        slot = final.at[other if back else own]
        return remote(slot, slot, end_send.at[d], end_recv.at[d], {"seq": cell + other})

    each(1, groups_chan, lambda d: middle(d).start())
    inner(half, blocks)

    def edge_arrived(d):
        source = lax.rem(place + parts - d, parts)
        for i in range(local - per):
            edge_copy(source, place, turn(i), d, {"seq": source}).wait_recv()

    each(1, parts, edge_arrived)

    def outputs(first, last):
        if first == last:
            return

        @pl.loop(first, last)
        def _(block):
            fb = lax.rem(block, local)
            rep = block // local
            fl = filter_lanes(fb, cols, filters)
            carry_block(rows, fb, rep, fl, edges, logr, carry)
            output_block(
                scale, fl, res, logr, conv.at[block], grad.at[block], xs.at[block], ys.at[block], carry, a_s, p_s, q_s
            )
            d = grad[block]
            at = block_lanes(block)
            out_sig[:, at] = (d * ins[1, block].astype(f32)).astype(bf16)
            out_gate[:, at] = (d * ins[0, block].astype(f32)).astype(bf16)
            out_outer[:, at] = (conv[block] * ins[3, block].astype(f32)).astype(bf16)

    stop = blocks * 5 // 8
    outputs(0, stop)
    each(1, groups_chan, lambda d: middle(d, back=True).wait_recv())
    for kind in range(kinds):
        total = slots[kind].astype(f32)
        for source in range(kind + kinds, groups_chan, kinds):
            total = total + slots[source].astype(f32)
        final[own, kind] = norm * total
    each(1, owners, lambda d: ending(d).start())
    outputs(stop, blocks)
    each(1, owners, lambda d: ending(d, back=True).wait_recv())
    for owner in range(owners):
        for kind in range(kinds):
            for i in range(per):
                first = (kind * local + owner * per + i) * LANES
                for which in range(2):
                    sums[which, :, first : first + LANES] = final[owner, kind, i, which]

    def edge_sent(d):
        other = lax.rem(place + d, parts)
        whose = lax.rem(other, owners)
        for i in range(local):
            fb = lax.rem(whose * per + i, local)
            if i < per:
                piece_copy(place, fb, d, {"seq": other}).wait_send()
            else:
                edge_copy(place, other, fb, d, {"seq": other}).wait_send()

    each(1, parts, edge_sent)
    each(1, groups_chan, lambda d: middle(d).wait_send())
    each(1, owners, lambda d: ending(d).wait_send())


def pass_kernel(sig, gate, outer, sums, out_sig, out_gate, out_outer, out_res, out_rate, sem):
    pairs = ((sig, out_sig), (gate, out_gate), (outer, out_outer), (sums.at[0], out_res), (sums.at[1], out_rate))
    copies = [pltpu.make_async_copy(src, dst, sem.at[n]) for n, (src, dst) in enumerate(pairs)]
    for copy in copies:
        copy.start()
    for copy in copies:
        copy.wait()


def on_device(signal_in, gate_in, outer_gate, cotangent, residues, log_rates):
    parts = lax.axis_size("seq")
    groups_chan = lax.axis_size("chan")
    rows, cols = signal_in.shape
    modes, filters = residues.shape
    total = parts * rows
    blocks = cols // LANES
    segs = rows // SEG
    local = min(cols, filters) // LANES
    owners = math.gcd(parts, local)
    per = local // owners
    kinds = filters // LANES // local
    reps = blocks // local
    scale = float(total) ** (-0.5)
    norm = float(total * cols * groups_chan // filters) ** (-0.5)
    whole = pl.BlockSpec(memory_space=pltpu.VMEM)
    far = pl.BlockSpec(memory_space=pl.ANY)
    shape = jax.ShapeDtypeStruct
    tiles = pltpu.VMEM((blocks, rows, LANES), f32)
    states = pltpu.VMEM((blocks, segs * modes, LANES), f32)
    phases = pltpu.VMEM((reps, segs // PACK, SEG * PACK, LANES), bf16)
    dma = pltpu.SemaphoreType.DMA
    narrow = shape((rows, cols), bf16)
    near = pltpu.VMEM((rows, cols), bf16)
    results = pl.pallas_call(
        functools.partial(whole_kernel, scale, norm, parts, groups_chan, owners),
        out_shape=(near, near, near, pltpu.VMEM((2, modes, filters), f32)),
        in_specs=[pl.BlockSpec(memory_space=pltpu.HBM)] * 6,
        out_specs=(whole,) * 4,
        scratch_shapes=[
            pltpu.VMEM((4, blocks, rows, LANES), bf16),
            pltpu.VMEM((2, modes, filters), f32),
            tiles,
            tiles,
            tiles,
            tiles,
            states,
            states,
            pltpu.VMEM((parts, local, 4 * reps + 2, modes, LANES), bf16),
            pltpu.VMEM((2, modes, LANES), f32),
            pltpu.VMEM((local, SEG, LANES), f32),
            phases,
            phases,
            pltpu.VMEM((modes, LANES), f32),
            pltpu.VMEM(((SEG + 1) * modes, LANES), f32),
            pltpu.VMEM((reps, 4, modes * segs, LANES), f32),
            pltpu.VMEM((SEG * SUB, LANES), f32),
            pltpu.VMEM((segs * modes, LANES), f32),
            pltpu.VMEM((segs * modes, LANES), f32),
            pltpu.VMEM((groups_chan, per, 2, modes, LANES), bf16),
            pltpu.VMEM((owners, kinds, per, 2, modes, LANES), f32),
            dma((4, blocks)),
            dma((2,)),
            dma((parts, local)),
            dma((parts, local)),
            dma((groups_chan,)),
            dma((groups_chan,)),
            dma((owners,)),
            dma((owners,)),
        ],
        compiler_params=pltpu.CompilerParams(
            collective_id=0, has_side_effects=True
        ),
        name="whole",
    )(signal_in, gate_in, outer_gate, cotangent, residues, log_rates)
    results = [pltpu.with_memory_space_constraint(a, pltpu.VMEM) for a in results]
    return pl.pallas_call(
        pass_kernel,
        out_shape=(narrow, narrow, narrow, shape((modes, filters), f32), shape((modes, filters), f32)),
        in_specs=[whole] * 4,
        out_specs=(far,) * 5,
        scratch_shapes=[dma((5,))],
        name="passed",
    )(*results)


def solution(mesh):
    placed = (P("seq", "chan"), P("seq", "chan"), P("seq", "chan"), P("seq", "chan"), P(), P())
    return jax.shard_map(
        on_device,
        mesh=mesh,
        in_specs=placed,
        out_specs=(P("seq", "chan"), P("seq", "chan"), P("seq", "chan"), P(), P()),
        check_vma=False,
    )
```

```python
import functools
import math

import jax
import jax.numpy as jnp
from jax import lax
from jax.experimental import pallas as pl
from jax.experimental.pallas import tpu as pltpu
from jax.sharding import PartitionSpec as P

LANES = 128
SUB = 8
SEG = 16
PACK = 16
PITCH = SEG + 1
f32 = jnp.float32
bf16 = jnp.bfloat16
MESH = pl.DeviceIdType.MESH


def rows_of(ref, first, stride):
    return ref[pl.ds(first, SUB, stride=stride), :]


def spread(ref, row):
    return jnp.broadcast_to(ref[pl.ds(row, 1), :], (SUB, LANES))


def spread_narrow(ref, row):
    return jnp.broadcast_to(ref[pl.ds(row, 1), :], (PACK, LANES)).astype(bf16)


def block_lanes(block):
    return pl.ds(pl.multiple_of(block * LANES, LANES), LANES)


def filter_lanes(block, cols, filters):
    start = lax.axis_index("chan") * cols + block * LANES
    return pl.ds(pl.multiple_of(lax.rem(start, filters), LANES), LANES)


def tree(values):
    while len(values) > 1:
        paired = [values[i] + values[i + 1] for i in range(0, len(values) - 1, 2)]
        values = paired + values[len(paired) * 2 :]
    return values[0]


def moments(terms, last):
    quads, weighted = [], []
    for first in range(0, len(terms), 4):
        p = [terms[first]]
        for term in terms[first + 1 : first + 4]:
            p.append(p[-1] + term)
        quads.append(p[-1])
        weighted.append(tree(p if last else p[:3]))
    q = [quads[0]]
    for quad in quads[1:]:
        q.append(q[-1] + quad)
    return q[-1], tree(weighted) + 4.0 * tree(q[:-1])


def state_block(scale, place, fb, local, fl, ins, res, logr, g_s, w_s, gt, wt, h_s, pw_s, less_s, plain, st, lag_s, xs, ys,
                edges):
    modes = res.shape[0]
    segs = g_s.shape[1] // PITCH
    hop = segs + 1
    reps = g_s.shape[0] // local
    rate = jnp.exp(logr[:, fl])
    amp = res[:, fl] * scale
    a = jnp.exp(-rate)
    power = jnp.ones((modes, LANES), f32)
    for u in range(SEG + 1):
        pw_s[u * modes : (u + 1) * modes, :] = power
        less_s[u * modes : (u + 1) * modes, :] = power - 1.0
        if u < SEG:
            h_s[fb, u : u + 1, :] = jnp.sum(amp * power, 0, keepdims=True)
            power = power * a
    seg_decay = power

    for rep in range(reps):
        block = rep * local + fb
        sig, gate, outer, cot = (ins[i, block].astype(f32) for i in range(4))
        g = (sig * gate).astype(bf16).astype(f32)
        w = (cot * outer).astype(bf16).astype(f32)
        for seg in range(segs):
            g_s[block, seg * PITCH : seg * PITCH + SEG, :] = g[seg * SEG : (seg + 1) * SEG]
            w_s[block, seg * PITCH : seg * PITCH + SEG, :] = w[seg * SEG : (seg + 1) * SEG]
        for i, (src, dst) in enumerate(((g_s.at[block], gt), (w_s.at[block], wt))):
            for part in range(segs // PACK):
                base = part * PACK * PITCH
                running = jnp.zeros((PACK, LANES), f32)
                weighted = running
                for j in range(SEG) if i == 0 else reversed(range(SEG)):
                    halves = [rows_of(src, base + half * SUB * PITCH + j, PITCH) for half in range(PACK // SUB)]
                    value = jnp.concatenate(halves, 0)
                    dst[rep, part, j * PACK : (j + 1) * PACK, :] = value.astype(bf16)
                    running = running + value
                    if i == 0 or j > 0:
                        weighted = weighted + running
                at = slice(part * PACK, (part + 1) * PACK)
                plain[rep, 2 * i, at, :] = running
                plain[rep, 2 * i + 1, at, :] = weighted

    def phase(ref, rep, part, j):
        return ref[rep, part, j * PACK : (j + 1) * PACK, :]

    for k in range(modes):
        powers = [spread_narrow(less_s, e * modes + k) for e in range(1, SEG + 1)]
        for rep in range(reps):
            for part in range(segs // PACK):
                x, d = moments([powers[SEG - 1 - j] * phase(gt, rep, part, j) for j in range(SEG)], True)
                y, v = moments([powers[j - 1] * phase(wt, rep, part, j) for j in range(SEG - 1, 0, -1)], False)
                rows = slice(part * PACK, (part + 1) * PACK)
                at = slice(k * hop + part * PACK, k * hop + (part + 1) * PACK)
                for i, value in enumerate((x, d, y, v)):
                    st[rep, i, at, :] = plain[rep, i, rows, :] + value.astype(f32)

    lags = [None] * SEG
    for rep in range(reps):
        for part in range(segs // PACK):
            g = [phase(gt, rep, part, j) for j in range(SEG)]
            w = [phase(wt, rep, part, j) for j in range(SEG)]
            for u in range(SEG):
                total = tree([w[j] * g[j - u] for j in range(u, SEG)]).astype(f32)
                total = total[:SUB] + total[SUB:]
                if rep + part == 0:
                    lag_s[u * SUB : (u + 1) * SUB, :] = total
                else:
                    lag_s[u * SUB : (u + 1) * SUB, :] += total

    gr = jnp.zeros((modes, LANES), f32)
    gl = jnp.zeros((modes, LANES), f32)
    for u in range(SEG):
        total = jnp.sum(lag_s[u * SUB : (u + 1) * SUB, :], 0, keepdims=True)
        term = total * pw_s[u * modes : (u + 1) * modes, :]
        gr = gr + term
        if u > 0:
            gl = gl + float(u) * term
    zero = jnp.zeros((modes, LANES), f32)
    for rep in range(reps):
        block = rep * local + fb
        x, xd = zero, zero
        for seg in range(segs):
            at = pl.ds(seg, modes, stride=hop)
            e, d, y, v = (st[rep, i, at, :] for i in range(4))
            xs[block, seg * modes : (seg + 1) * modes, :] = x
            if seg > 0:
                gr = gr + x * y
                gl = gl + (xd * y + x * v)
            xd = seg_decay * (xd + float(SEG) * x) + d
            x = seg_decay * x + e
        y, yv = zero, zero
        for seg in reversed(range(segs)):
            at = pl.ds(seg, modes, stride=hop)
            ys[block, seg * modes : (seg + 1) * modes, :] = y
            yv = st[rep, 3, at, :] + seg_decay * (yv + float(SEG) * y)
            y = st[rep, 2, at, :] + seg_decay * y
        for i, value in enumerate((x, y, xd, yv)):
            edges[place, fb, i * reps + rep] = value.astype(bf16)
    edges[place, fb, 4 * reps] = gr.astype(bf16)
    edges[place, fb, 4 * reps + 1] = gl.astype(bf16)


def inner_block(g_s, w_s, h_s, conv, grad):
    @pl.loop(0, g_s.shape[0] // (PITCH * SUB))
    def _(group):
        base = group * (SUB * PITCH)
        h = [spread(h_s, u) for u in range(SEG)]
        g = [rows_of(g_s, base + j, PITCH) for j in range(SEG)]
        for j in range(SEG):
            forward = h[0] * g[j]
            for u in range(1, j + 1):
                forward = forward + h[u] * g[j - u]
            conv[pl.ds(base + j, SUB, stride=PITCH), :] = forward
        w = [rows_of(w_s, base + j, PITCH) for j in range(SEG)]
        for j in range(SEG):
            backward = h[0] * w[j]
            for u in range(1, SEG - j):
                backward = backward + h[u] * w[j + u]
            grad[pl.ds(base + j, SUB, stride=PITCH), :] = backward


def gradient_block(scale, span, fb, fl, edges, res, logr):
    parts = edges.shape[0]
    reps = edges.shape[2] // 4
    rate = jnp.exp(logr[:, fl])
    decay = jnp.exp(-rate * float(span))

    def value(source, i):
        return edges[source, fb, i].astype(f32)

    gr = tree([value(source, 4 * reps) for source in range(parts)])
    gl = tree([value(source, 4 * reps + 1) for source in range(parts)])
    for rep in range(reps):
        x = value(0, rep)
        xd = value(0, 2 * reps + rep)
        for source in range(1, parts):
            y = value(source, reps + rep)
            gr = gr + x * y
            gl = gl + (x * value(source, 3 * reps + rep) + xd * y)
            if source < parts - 1:
                xd = (xd + float(span) * x) * decay + value(source, 2 * reps + rep)
                x = x * decay + value(source, rep)
    return scale * gr, -scale * (res[:, fl] * rate) * gl


def carry_block(span, fb, rep, fl, edges, logr, carry):
    place = lax.axis_index("seq")
    parts = edges.shape[0]
    reps = edges.shape[2] // 4
    decay = jnp.exp(-jnp.exp(logr[:, fl]) * float(span))
    values = []
    for source in range(parts):
        which = jnp.where(source > place, reps, 0)
        values.append(edges[source, fb, which + rep].astype(f32))
    x = jnp.zeros(decay.shape, f32)
    y = x
    for source in range(parts):
        x = jnp.where(source < place, x * decay + values[source], x)
        back = parts - 1 - source
        y = jnp.where(back > place, y * decay + values[back], y)
    carry[0] = x
    carry[1] = y


def output_block(scale, fl, res, logr, conv, grad, xs, ys, carry, a_s, p_s, q_s):
    modes = res.shape[0]
    segs = conv.shape[0] // PITCH
    hop = modes + 1
    rate = jnp.exp(logr[:, fl])
    amp = res[:, fl] * scale
    a_s[...] = jnp.exp(-rate)
    seg_decay = jnp.exp(-rate * float(SEG))
    p = amp * carry[0]
    q = amp * carry[1]
    for seg in range(segs):
        p_s[seg * hop : seg * hop + modes, :] = amp * xs[seg * modes : (seg + 1) * modes, :] + p
        p = p * seg_decay
        back = segs - 1 - seg
        q_s[back * hop : back * hop + modes, :] = amp * ys[back * modes : (back + 1) * modes, :] + q
        q = q * seg_decay

    @pl.loop(0, segs // SUB)
    def _(group):
        base = group * (SUB * PITCH)
        for half in range(0, modes, SUB):
            decay = [spread(a_s, half + k) for k in range(SUB)]
            p = [rows_of(p_s, group * (SUB * hop) + half + k, hop) for k in range(SUB)]
            q = [rows_of(q_s, group * (SUB * hop) + half + k, hop) for k in range(SUB)]
            for j in range(SEG):
                at = pl.ds(base + j, SUB, stride=PITCH)
                conv[at, :] = conv[at, :] + tree(p)
                q = [decay[k] * q[k] for k in range(SUB)]
                at = pl.ds(base + SEG - 1 - j, SUB, stride=PITCH)
                grad[at, :] = grad[at, :] + tree(q)
                if j < SEG - 1:
                    p = [decay[k] * p[k] for k in range(SUB)]


def whole_kernel(
    scale, norm, parts, groups_chan, owners,
    sig_h, gate_h, outer_h, cot_h, res_h, logr_h,
    out_sig, out_gate, out_outer, sums,
    ins, params, g_s, w_s, conv, grad, xs, ys, edges, carry, h_s, gt, wt,
    a_s, pw_s, less_s, plain, st, lag_s, p_s, q_s, slots, final,
    in_sem, param_sem, edge_send, edge_recv, mid_send, mid_recv, end_send, end_recv,
):
    rows, cols = sig_h.shape
    modes, filters = res_h.shape
    blocks = cols // LANES
    local = edges.shape[1]
    reps = blocks // local
    per = local // owners
    kinds = final.shape[1]
    place = lax.axis_index("seq")
    column = lax.axis_index("chan")
    own = lax.rem(place, owners)
    cell = place - own
    barrier = pltpu.get_barrier_semaphore()

    def each(first, last, fn):
        if last - first <= 8:
            for d in range(first, last):
                fn(d)
        else:
            pl.loop(first, last)(fn)

    def remote(src, dst, send, recv, device):
        return pltpu.make_async_remote_copy(
            src_ref=src, dst_ref=dst, send_sem=send, recv_sem=recv, device_id=device, device_id_type=MESH
        )

    def greet(axis, index, size):
        def signal(d):
            other = lax.rem(index + d, size)
            pl.semaphore_signal(barrier, inc=1, device_id={axis: other}, device_id_type=MESH)

        each(1, size, signal)

    greet("chan", column, groups_chan)
    greet("seq", place, parts)

    param_copies = [
        pltpu.make_async_copy(ref, params.at[i], param_sem.at[i]) for i, ref in enumerate((res_h, logr_h))
    ]
    for copy in param_copies:
        copy.start()

    def fetch(i, ref, block):
        return pltpu.make_async_copy(ref.at[:, block_lanes(block)], ins.at[i, block], in_sem.at[i, block])

    whole_inputs = (sig_h, gate_h, outer_h, cot_h)

    def turn(i):
        return lax.rem(own * per + per + i, local)

    @pl.loop(0, local)
    def _(i):
        for rep in range(reps):
            for n, ref in enumerate(whole_inputs):
                fetch(n, ref, rep * local + turn(i)).start()

    for copy in param_copies:
        copy.wait()
    res, logr = params.at[0], params.at[1]

    def piece_copy(sender, fb, d, device):
        ref = edges.at[sender, fb]
        return remote(ref, ref, edge_send.at[d, fb], edge_recv.at[d, fb], device)

    def edge_copy(sender, receiver, fb, d, device):
        first = jnp.where(receiver > sender, 0, reps)
        ref = edges.at[sender, fb, pl.ds(first, reps)]
        return remote(ref, ref, edge_send.at[d, fb], edge_recv.at[d, fb], device)

    @pl.loop(0, local)
    def _(i):
        fb = turn(i)
        for rep in range(reps):
            for n, ref in enumerate(whole_inputs):
                fetch(n, ref, rep * local + fb).wait()
        state_block(
            scale, place, fb, local, filter_lanes(fb, cols, filters), ins, res, logr, g_s, w_s, gt, wt, h_s, pw_s,
            less_s, plain, st, lag_s, xs, ys, edges,
        )

        @pl.when(i == 0)
        def _():
            pl.semaphore_wait(barrier, parts - 1 + groups_chan - 1)

        def send(d):
            other = lax.rem(place + d, parts)
            whose = lax.rem(other, owners)
            is_piece = jnp.logical_and(fb >= whose * per, fb < (whose + 1) * per)

            @pl.when(is_piece)
            def _():
                piece_copy(place, fb, d, {"seq": other}).start()

            @pl.when(jnp.logical_not(is_piece))
            def _():
                edge_copy(place, other, fb, d, {"seq": other}).start()

        each(1, parts, send)

    def inner(first, last):
        if first == last:
            return

        @pl.loop(first, last)
        def _(block):
            fb = lax.rem(block, local)
            inner_block(g_s.at[block], w_s.at[block], h_s.at[fb], conv.at[block], grad.at[block])

    half = blocks // 2
    inner(0, half)

    def piece_arrived(d):
        source = lax.rem(place + parts - d, parts)
        for i in range(per):
            piece_copy(source, own * per + i, d, {"seq": source}).wait_recv()

    each(1, parts, piece_arrived)
    for i in range(per):
        fb = own * per + i
        first, second = gradient_block(scale, rows, fb, filter_lanes(fb, cols, filters), edges, res, logr)
        slots[column, i, 0] = first.astype(bf16)
        slots[column, i, 1] = second.astype(bf16)

    def middle(d, back=False):
        other = lax.rem(column + (groups_chan - d if back else d), groups_chan)
        slot = slots.at[other if back else column]
        return remote(slot, slot, mid_send.at[d], mid_recv.at[d], {"chan": other})

    def ending(d, back=False):
        other = lax.rem(own + (owners - d if back else d), owners)
        slot = final.at[other if back else own]
        return remote(slot, slot, end_send.at[d], end_recv.at[d], {"seq": cell + other})

    each(1, groups_chan, lambda d: middle(d).start())
    inner(half, blocks)

    def edge_arrived(d):
        source = lax.rem(place + parts - d, parts)
        for i in range(local - per):
            edge_copy(source, place, turn(i), d, {"seq": source}).wait_recv()

    each(1, parts, edge_arrived)

    def outputs(first, last):
        if first == last:
            return

        @pl.loop(first, last)
        def _(block):
            fb = lax.rem(block, local)
            rep = block // local
            fl = filter_lanes(fb, cols, filters)
            carry_block(rows, fb, rep, fl, edges, logr, carry)
            output_block(
                scale, fl, res, logr, conv.at[block], grad.at[block], xs.at[block], ys.at[block], carry, a_s, p_s, q_s
            )
            at = block_lanes(block)
            for seg in range(rows // SEG):
                own_rows = slice(seg * SEG, (seg + 1) * SEG)
                d = grad[block, seg * PITCH : seg * PITCH + SEG, :]
                c = conv[block, seg * PITCH : seg * PITCH + SEG, :]
                out_sig[own_rows, at] = (d * ins[1, block, own_rows, :].astype(f32)).astype(bf16)
                out_gate[own_rows, at] = (d * ins[0, block, own_rows, :].astype(f32)).astype(bf16)
                out_outer[own_rows, at] = (c * ins[3, block, own_rows, :].astype(f32)).astype(bf16)

    stop = blocks * 5 // 8
    outputs(0, stop)
    each(1, groups_chan, lambda d: middle(d, back=True).wait_recv())
    for kind in range(kinds):
        total = slots[kind].astype(f32)
        for source in range(kind + kinds, groups_chan, kinds):
            total = total + slots[source].astype(f32)
        final[own, kind] = norm * total
    each(1, owners, lambda d: ending(d).start())
    outputs(stop, blocks)
    each(1, owners, lambda d: ending(d, back=True).wait_recv())
    for owner in range(owners):
        for kind in range(kinds):
            for i in range(per):
                first = (kind * local + owner * per + i) * LANES
                for which in range(2):
                    sums[which, :, first : first + LANES] = final[owner, kind, i, which]

    def edge_sent(d):
        other = lax.rem(place + d, parts)
        whose = lax.rem(other, owners)
        for i in range(local):
            fb = lax.rem(whose * per + i, local)
            if i < per:
                piece_copy(place, fb, d, {"seq": other}).wait_send()
            else:
                edge_copy(place, other, fb, d, {"seq": other}).wait_send()

    each(1, parts, edge_sent)
    each(1, groups_chan, lambda d: middle(d).wait_send())
    each(1, owners, lambda d: ending(d).wait_send())


def pass_kernel(sig, gate, outer, sums, out_sig, out_gate, out_outer, out_res, out_rate, sem):
    pairs = ((sig, out_sig), (gate, out_gate), (outer, out_outer), (sums.at[0], out_res), (sums.at[1], out_rate))
    copies = [pltpu.make_async_copy(src, dst, sem.at[n]) for n, (src, dst) in enumerate(pairs)]
    for copy in copies:
        copy.start()
    for copy in copies:
        copy.wait()


def on_device(signal_in, gate_in, outer_gate, cotangent, residues, log_rates):
    parts = lax.axis_size("seq")
    groups_chan = lax.axis_size("chan")
    rows, cols = signal_in.shape
    modes, filters = residues.shape
    total = parts * rows
    blocks = cols // LANES
    segs = rows // SEG
    local = min(cols, filters) // LANES
    owners = math.gcd(parts, local)
    per = local // owners
    kinds = filters // LANES // local
    reps = blocks // local
    scale = float(total) ** (-0.5)
    norm = float(total * cols * groups_chan // filters) ** (-0.5)
    whole = pl.BlockSpec(memory_space=pltpu.VMEM)
    far = pl.BlockSpec(memory_space=pl.ANY)
    shape = jax.ShapeDtypeStruct
    tiles = pltpu.VMEM((blocks, segs * PITCH, LANES), f32)
    states = pltpu.VMEM((blocks, segs * modes, LANES), f32)
    phases = pltpu.VMEM((reps, segs // PACK, SEG * PACK, LANES), bf16)
    dma = pltpu.SemaphoreType.DMA
    narrow = shape((rows, cols), bf16)
    near = pltpu.VMEM((rows, cols), bf16)
    results = pl.pallas_call(
        functools.partial(whole_kernel, scale, norm, parts, groups_chan, owners),
        out_shape=(near, near, near, pltpu.VMEM((2, modes, filters), f32)),
        in_specs=[pl.BlockSpec(memory_space=pltpu.HBM)] * 6,
        out_specs=(whole,) * 4,
        scratch_shapes=[
            pltpu.VMEM((4, blocks, rows, LANES), bf16),
            pltpu.VMEM((2, modes, filters), f32),
            tiles,
            tiles,
            tiles,
            tiles,
            states,
            states,
            pltpu.VMEM((parts, local, 4 * reps + 2, modes, LANES), bf16),
            pltpu.VMEM((2, modes, LANES), f32),
            pltpu.VMEM((local, SEG, LANES), f32),
            phases,
            phases,
            pltpu.VMEM((modes, LANES), f32),
            pltpu.VMEM(((SEG + 1) * modes, LANES), f32),
            pltpu.VMEM(((SEG + 1) * modes, LANES), f32),
            pltpu.VMEM((reps, 4, segs, LANES), f32),
            pltpu.VMEM((reps, 4, modes * (segs + 1), LANES), f32),
            pltpu.VMEM((SEG * SUB, LANES), f32),
            pltpu.VMEM((segs * (modes + 1), LANES), f32),
            pltpu.VMEM((segs * (modes + 1), LANES), f32),
            pltpu.VMEM((groups_chan, per, 2, modes, LANES), bf16),
            pltpu.VMEM((owners, kinds, per, 2, modes, LANES), f32),
            dma((4, blocks)),
            dma((2,)),
            dma((parts, local)),
            dma((parts, local)),
            dma((groups_chan,)),
            dma((groups_chan,)),
            dma((owners,)),
            dma((owners,)),
        ],
        compiler_params=pltpu.CompilerParams(
            collective_id=0, has_side_effects=True
        ),
        name="whole",
    )(signal_in, gate_in, outer_gate, cotangent, residues, log_rates)
    results = [pltpu.with_memory_space_constraint(a, pltpu.VMEM) for a in results]
    return pl.pallas_call(
        pass_kernel,
        out_shape=(narrow, narrow, narrow, shape((modes, filters), f32), shape((modes, filters), f32)),
        in_specs=[whole] * 4,
        out_specs=(far,) * 5,
        scratch_shapes=[dma((5,))],
        name="passed",
    )(*results)


def solution(mesh):
    placed = (P("seq", "chan"), P("seq", "chan"), P("seq", "chan"), P("seq", "chan"), P(), P())
    return jax.shard_map(
        on_device,
        mesh=mesh,
        in_specs=placed,
        out_specs=(P("seq", "chan"), P("seq", "chan"), P("seq", "chan"), P(), P()),
        check_vma=False,
    )
```

```python
import functools
import math

import jax
import jax.numpy as jnp
from jax import lax
from jax.experimental import pallas as pl
from jax.experimental.pallas import tpu as pltpu
from jax.sharding import PartitionSpec as P

LANES = 128
SUB = 8
SEG = 16
PACK = 16
PITCH = SEG + 1
f32 = jnp.float32
bf16 = jnp.bfloat16
MESH = pl.DeviceIdType.MESH


def rows_of(ref, first, stride):
    return ref[pl.ds(first, SUB, stride=stride), :]


def spread(ref, row):
    return jnp.broadcast_to(ref[pl.ds(row, 1), :], (SUB, LANES))


def spread_narrow(ref, row):
    return jnp.broadcast_to(ref[pl.ds(row, 1), :], (PACK, LANES)).astype(bf16)


def block_lanes(block):
    return pl.ds(pl.multiple_of(block * LANES, LANES), LANES)


def filter_lanes(block, cols, filters):
    start = lax.axis_index("chan") * cols + block * LANES
    return pl.ds(pl.multiple_of(lax.rem(start, filters), LANES), LANES)


def tree(values):
    while len(values) > 1:
        paired = [values[i] + values[i + 1] for i in range(0, len(values) - 1, 2)]
        values = paired + values[len(paired) * 2 :]
    return values[0]


def moments(terms, last):
    quads, weighted = [], []
    for first in range(0, len(terms), 4):
        p = [terms[first]]
        for term in terms[first + 1 : first + 4]:
            p.append(p[-1] + term)
        quads.append(p[-1])
        weighted.append(tree(p if last else p[:3]))
    q = [quads[0]]
    for quad in quads[1:]:
        q.append(q[-1] + quad)
    return q[-1], tree(weighted) + 4.0 * tree(q[:-1])


def state_block(scale, place, fb, local, fl, ins, res, logr, g_s, w_s, gt, wt, h_s, pw_s, less_s, plain, st, lag_s, xs, ys,
                edges):
    modes = res.shape[0]
    segs = g_s.shape[1] // PITCH
    hop = segs + 1
    reps = g_s.shape[0] // local
    rate = jnp.exp(logr[:, fl])
    amp = res[:, fl] * scale
    a = jnp.exp(-rate)
    power = jnp.ones((modes, LANES), f32)
    for u in range(SEG + 1):
        pw_s[u * modes : (u + 1) * modes, :] = power
        less_s[u * modes : (u + 1) * modes, :] = power - 1.0
        if u < SEG:
            h_s[fb, u : u + 1, :] = jnp.sum(amp * power, 0, keepdims=True)
            power = power * a
    seg_decay = power

    for rep in range(reps):
        block = rep * local + fb
        g = (ins[0, block] * ins[1, block]).astype(f32)
        w = (ins[3, block] * ins[2, block]).astype(f32)
        for seg in range(segs):
            g_s[block, seg * PITCH : seg * PITCH + SEG, :] = g[seg * SEG : (seg + 1) * SEG]
            w_s[block, seg * PITCH : seg * PITCH + SEG, :] = w[seg * SEG : (seg + 1) * SEG]
        for i, (src, dst) in enumerate(((g_s.at[block], gt), (w_s.at[block], wt))):
            for part in range(segs // PACK):
                base = part * PACK * PITCH
                running = jnp.zeros((PACK, LANES), f32)
                weighted = running
                for j in range(SEG) if i == 0 else reversed(range(SEG)):
                    halves = [rows_of(src, base + half * SUB * PITCH + j, PITCH) for half in range(PACK // SUB)]
                    value = jnp.concatenate(halves, 0)
                    dst[rep, part, j * PACK : (j + 1) * PACK, :] = value.astype(bf16)
                    running = running + value
                    if i == 0 or j > 0:
                        weighted = weighted + running
                at = slice(part * PACK, (part + 1) * PACK)
                plain[rep, 2 * i, at, :] = running
                plain[rep, 2 * i + 1, at, :] = weighted

    def phase(ref, rep, part, j):
        return ref[rep, part, j * PACK : (j + 1) * PACK, :]

    for k in range(modes):
        powers = [spread_narrow(less_s, e * modes + k) for e in range(1, SEG + 1)]
        for rep in range(reps):
            for part in range(segs // PACK):
                x, d = moments([powers[SEG - 1 - j] * phase(gt, rep, part, j) for j in range(SEG)], True)
                y, v = moments([powers[j - 1] * phase(wt, rep, part, j) for j in range(SEG - 1, 0, -1)], False)
                rows = slice(part * PACK, (part + 1) * PACK)
                at = slice(k * hop + part * PACK, k * hop + (part + 1) * PACK)
                for i, value in enumerate((x, d, y, v)):
                    st[rep, i, at, :] = plain[rep, i, rows, :] + value.astype(f32)

    lags = [None] * SEG
    for rep in range(reps):
        for part in range(segs // PACK):
            g = [phase(gt, rep, part, j) for j in range(SEG)]
            w = [phase(wt, rep, part, j) for j in range(SEG)]
            for u in range(SEG):
                total = tree([w[j] * g[j - u] for j in range(u, SEG)]).astype(f32)
                total = total[:SUB] + total[SUB:]
                if rep + part == 0:
                    lag_s[u * SUB : (u + 1) * SUB, :] = total
                else:
                    lag_s[u * SUB : (u + 1) * SUB, :] += total

    gr = jnp.zeros((modes, LANES), f32)
    gl = jnp.zeros((modes, LANES), f32)
    for u in range(SEG):
        total = jnp.sum(lag_s[u * SUB : (u + 1) * SUB, :], 0, keepdims=True)
        term = total * pw_s[u * modes : (u + 1) * modes, :]
        gr = gr + term
        if u > 0:
            gl = gl + float(u) * term
    zero = jnp.zeros((modes, LANES), f32)
    for rep in range(reps):
        block = rep * local + fb
        x, xd = zero, zero
        for seg in range(segs):
            at = pl.ds(seg, modes, stride=hop)
            e, d, y, v = (st[rep, i, at, :] for i in range(4))
            xs[block, seg * modes : (seg + 1) * modes, :] = x
            if seg > 0:
                gr = gr + x * y
                gl = gl + (xd * y + x * v)
            xd = seg_decay * (xd + float(SEG) * x) + d
            x = seg_decay * x + e
        y, yv = zero, zero
        for seg in reversed(range(segs)):
            at = pl.ds(seg, modes, stride=hop)
            ys[block, seg * modes : (seg + 1) * modes, :] = y
            yv = st[rep, 3, at, :] + seg_decay * (yv + float(SEG) * y)
            y = st[rep, 2, at, :] + seg_decay * y
        for first, value in ((0, x), (reps, xd), (2 * reps + 2, y), (3 * reps + 2, yv)):
            edges[place, fb, first + rep] = value.astype(bf16)
    edges[place, fb, 2 * reps] = gr.astype(bf16)
    edges[place, fb, 2 * reps + 1] = gl.astype(bf16)


def inner_block(g_s, w_s, h_s, conv, grad):
    @pl.loop(0, g_s.shape[0] // (PITCH * SUB))
    def _(group):
        base = group * (SUB * PITCH)
        h = [spread(h_s, u) for u in range(SEG)]
        g = [rows_of(g_s, base + j, PITCH) for j in range(SEG)]
        for j in range(SEG):
            forward = h[0] * g[j]
            for u in range(1, j + 1):
                forward = forward + h[u] * g[j - u]
            conv[pl.ds(base + j, SUB, stride=PITCH), :] = forward
        w = [rows_of(w_s, base + j, PITCH) for j in range(SEG)]
        for j in range(SEG):
            backward = h[0] * w[j]
            for u in range(1, SEG - j):
                backward = backward + h[u] * w[j + u]
            grad[pl.ds(base + j, SUB, stride=PITCH), :] = backward


def gradient_block(scale, span, fb, fl, edges, res, logr):
    parts = edges.shape[0]
    reps = edges.shape[2] // 4
    rate = jnp.exp(logr[:, fl])
    decay = jnp.exp(-rate * float(span))

    def value(source, i):
        return edges[source, fb, i].astype(f32)

    gr = tree([value(source, 2 * reps) for source in range(parts)])
    gl = tree([value(source, 2 * reps + 1) for source in range(parts)])
    for rep in range(reps):
        x = value(0, rep)
        xd = value(0, reps + rep)
        for source in range(1, parts):
            y = value(source, 2 * reps + 2 + rep)
            gr = gr + x * y
            gl = gl + (x * value(source, 3 * reps + 2 + rep) + xd * y)
            if source < parts - 1:
                xd = (xd + float(span) * x) * decay + value(source, reps + rep)
                x = x * decay + value(source, rep)
    return scale * gr, -scale * (res[:, fl] * rate) * gl


def carry_block(span, fb, rep, fl, edges, logr, carry):
    place = lax.axis_index("seq")
    parts = edges.shape[0]
    reps = edges.shape[2] // 4
    decay = jnp.exp(-jnp.exp(logr[:, fl]) * float(span))
    values = []
    for source in range(parts):
        which = jnp.where(source > place, 2 * reps + 2, 0)
        values.append(edges[source, fb, which + rep].astype(f32))
    x = jnp.zeros(decay.shape, f32)
    y = x
    for source in range(parts):
        x = jnp.where(source < place, x * decay + values[source], x)
        back = parts - 1 - source
        y = jnp.where(back > place, y * decay + values[back], y)
    carry[0] = x
    carry[1] = y


def output_block(scale, fl, res, logr, conv, grad, xs, ys, carry, a_s, p_s, q_s):
    modes = res.shape[0]
    segs = conv.shape[0] // PITCH
    hop = modes + 1
    rate = jnp.exp(logr[:, fl])
    amp = res[:, fl] * scale
    a_s[...] = jnp.exp(-rate)
    seg_decay = jnp.exp(-rate * float(SEG))
    p = amp * carry[0]
    q = amp * carry[1]
    for seg in range(segs):
        p_s[seg * hop : seg * hop + modes, :] = amp * xs[seg * modes : (seg + 1) * modes, :] + p
        p = p * seg_decay
        back = segs - 1 - seg
        q_s[back * hop : back * hop + modes, :] = amp * ys[back * modes : (back + 1) * modes, :] + q
        q = q * seg_decay

    @pl.loop(0, segs // SUB)
    def _(group):
        base = group * (SUB * PITCH)
        for half in range(0, modes, SUB):
            decay = [spread(a_s, half + k) for k in range(SUB)]
            p = [rows_of(p_s, group * (SUB * hop) + half + k, hop) for k in range(SUB)]
            q = [rows_of(q_s, group * (SUB * hop) + half + k, hop) for k in range(SUB)]
            for j in range(SEG):
                at = pl.ds(base + j, SUB, stride=PITCH)
                conv[at, :] = conv[at, :] + tree(p)
                q = [decay[k] * q[k] for k in range(SUB)]
                at = pl.ds(base + SEG - 1 - j, SUB, stride=PITCH)
                grad[at, :] = grad[at, :] + tree(q)
                if j < SEG - 1:
                    p = [decay[k] * p[k] for k in range(SUB)]


def whole_kernel(
    scale, norm, parts, groups_chan, owners,
    sig_h, gate_h, outer_h, cot_h, res_h, logr_h,
    out_sig, out_gate, out_outer, sums,
    ins, params, g_s, w_s, conv, grad, xs, ys, edges, carry, h_s, gt, wt,
    a_s, pw_s, less_s, plain, st, lag_s, p_s, q_s, slots, final,
    in_sem, param_sem, edge_send, edge_recv, mid_send, mid_recv, end_send, end_recv,
):
    rows, cols = sig_h.shape
    modes, filters = res_h.shape
    blocks = cols // LANES
    local = edges.shape[1]
    reps = blocks // local
    per = local // owners
    kinds = final.shape[1]
    place = lax.axis_index("seq")
    column = lax.axis_index("chan")
    own = lax.rem(place, owners)
    cell = place - own
    barrier = pltpu.get_barrier_semaphore()

    def each(first, last, fn):
        if last - first <= 8:
            for d in range(first, last):
                fn(d)
        else:
            pl.loop(first, last)(fn)

    def remote(src, dst, send, recv, device):
        return pltpu.make_async_remote_copy(
            src_ref=src, dst_ref=dst, send_sem=send, recv_sem=recv, device_id=device, device_id_type=MESH
        )

    def greet(axis, index, size):
        def signal(d):
            other = lax.rem(index + d, size)
            pl.semaphore_signal(barrier, inc=1, device_id={axis: other}, device_id_type=MESH)

        each(1, size, signal)

    param_copies = [
        pltpu.make_async_copy(ref, params.at[i], param_sem.at[i]) for i, ref in enumerate((res_h, logr_h))
    ]
    for copy in param_copies:
        copy.start()

    def fetch(i, ref, block):
        return pltpu.make_async_copy(ref.at[:, block_lanes(block)], ins.at[i, block], in_sem.at[i, block])

    whole_inputs = (sig_h, gate_h, outer_h, cot_h)

    def turn(i):
        return lax.rem(own * per + per + i, local)

    @pl.loop(0, local)
    def _(i):
        for rep in range(reps):
            for n, ref in enumerate(whole_inputs):
                fetch(n, ref, rep * local + turn(i)).start()

    greet("chan", column, groups_chan)
    greet("seq", place, parts)

    for copy in param_copies:
        copy.wait()
    res, logr = params.at[0], params.at[1]

    def piece_copy(sender, fb, d, device, act):
        at_end = jnp.logical_or(sender == 0, sender == parts - 1)

        @pl.when(at_end)
        def _():
            ref = edges.at[sender, fb, pl.ds(jnp.where(sender == 0, 0, 2 * reps), 2 * reps + 2)]
            act(remote(ref, ref, edge_send.at[d, fb], edge_recv.at[d, fb], device))

        @pl.when(jnp.logical_not(at_end))
        def _():
            ref = edges.at[sender, fb]
            act(remote(ref, ref, edge_send.at[d, fb], edge_recv.at[d, fb], device))

    def edge_copy(sender, receiver, fb, d, device):
        first = jnp.where(receiver > sender, 0, 2 * reps + 2)
        ref = edges.at[sender, fb, pl.ds(first, reps)]
        return remote(ref, ref, edge_send.at[d, fb], edge_recv.at[d, fb], device)

    @pl.loop(0, local)
    def _(i):
        fb = turn(i)
        for rep in range(reps):
            for n, ref in enumerate(whole_inputs):
                fetch(n, ref, rep * local + fb).wait()
        state_block(
            scale, place, fb, local, filter_lanes(fb, cols, filters), ins, res, logr, g_s, w_s, gt, wt, h_s, pw_s,
            less_s, plain, st, lag_s, xs, ys, edges,
        )

        @pl.when(i == 0)
        def _():
            pl.semaphore_wait(barrier, parts - 1 + groups_chan - 1)

        def send(d):
            other = lax.rem(place + d, parts)
            whose = lax.rem(other, owners)
            is_piece = jnp.logical_and(fb >= whose * per, fb < (whose + 1) * per)

            @pl.when(is_piece)
            def _():
                piece_copy(place, fb, d, {"seq": other}, lambda copy: copy.start())

            @pl.when(jnp.logical_not(is_piece))
            def _():
                edge_copy(place, other, fb, d, {"seq": other}).start()

        each(1, parts, send)

    def inner(first, last):
        if first == last:
            return

        @pl.loop(first, last)
        def _(block):
            fb = lax.rem(block, local)
            inner_block(g_s.at[block], w_s.at[block], h_s.at[fb], conv.at[block], grad.at[block])

    half = blocks // 4
    inner(0, half)

    def piece_arrived(d):
        source = lax.rem(place + parts - d, parts)
        for i in range(per):
            piece_copy(source, own * per + i, d, {"seq": source}, lambda copy: copy.wait_recv())

    each(1, parts, piece_arrived)
    for i in range(per):
        fb = own * per + i
        first, second = gradient_block(scale, rows, fb, filter_lanes(fb, cols, filters), edges, res, logr)
        slots[column, i, 0] = first.astype(bf16)
        slots[column, i, 1] = second.astype(bf16)

    def middle(d, back=False):
        other = lax.rem(column + (groups_chan - d if back else d), groups_chan)
        slot = slots.at[other if back else column]
        return remote(slot, slot, mid_send.at[d], mid_recv.at[d], {"chan": other})

    def ending(d, back=False):
        other = lax.rem(own + (owners - d if back else d), owners)
        slot = final.at[other if back else own]
        return remote(slot, slot, end_send.at[d], end_recv.at[d], {"seq": cell + other})

    each(1, groups_chan, lambda d: middle(d).start())
    inner(half, blocks)

    def edge_arrived(d):
        source = lax.rem(place + parts - d, parts)
        for i in range(local - per):
            edge_copy(source, place, turn(i), d, {"seq": source}).wait_recv()

    each(1, parts, edge_arrived)

    def outputs(first, last):
        if first == last:
            return

        @pl.loop(first, last)
        def _(block):
            fb = lax.rem(block, local)
            rep = block // local
            fl = filter_lanes(fb, cols, filters)
            carry_block(rows, fb, rep, fl, edges, logr, carry)
            output_block(
                scale, fl, res, logr, conv.at[block], grad.at[block], xs.at[block], ys.at[block], carry, a_s, p_s, q_s
            )
            at = block_lanes(block)
            for seg in range(rows // SEG):
                own_rows = slice(seg * SEG, (seg + 1) * SEG)
                d = grad[block, seg * PITCH : seg * PITCH + SEG, :]
                c = conv[block, seg * PITCH : seg * PITCH + SEG, :]
                out_sig[own_rows, at] = (d * ins[1, block, own_rows, :].astype(f32)).astype(bf16)
                out_gate[own_rows, at] = (d * ins[0, block, own_rows, :].astype(f32)).astype(bf16)
                out_outer[own_rows, at] = (c * ins[3, block, own_rows, :].astype(f32)).astype(bf16)

    stop = blocks // 2
    outputs(0, stop)
    each(1, groups_chan, lambda d: middle(d, back=True).wait_recv())
    for kind in range(kinds):
        total = slots[kind].astype(f32)
        for source in range(kind + kinds, groups_chan, kinds):
            total = total + slots[source].astype(f32)
        final[own, kind] = (norm * total).astype(bf16)
    each(1, owners, lambda d: ending(d).start())
    outputs(stop, blocks)
    def edge_sent(d):
        other = lax.rem(place + d, parts)
        whose = lax.rem(other, owners)
        for i in range(local):
            fb = lax.rem(whose * per + i, local)
            if i < per:
                piece_copy(place, fb, d, {"seq": other}, lambda copy: copy.wait_send())
            else:
                edge_copy(place, other, fb, d, {"seq": other}).wait_send()

    each(1, parts, edge_sent)
    each(1, groups_chan, lambda d: middle(d).wait_send())
    each(1, owners, lambda d: ending(d, back=True).wait_recv())
    for owner in range(owners):
        for kind in range(kinds):
            for i in range(per):
                first = (kind * local + owner * per + i) * LANES
                for which in range(2):
                    sums[which, :, first : first + LANES] = final[owner, kind, i, which].astype(f32)

    each(1, owners, lambda d: ending(d).wait_send())


def pass_kernel(sig, gate, outer, sums, out_sig, out_gate, out_outer, out_res, out_rate, sem):
    pairs = ((sig, out_sig), (gate, out_gate), (outer, out_outer), (sums.at[0], out_res), (sums.at[1], out_rate))
    copies = [pltpu.make_async_copy(src, dst, sem.at[n]) for n, (src, dst) in enumerate(pairs)]
    for copy in copies:
        copy.start()
    for copy in copies:
        copy.wait()


def on_device(signal_in, gate_in, outer_gate, cotangent, residues, log_rates):
    parts = lax.axis_size("seq")
    groups_chan = lax.axis_size("chan")
    rows, cols = signal_in.shape
    modes, filters = residues.shape
    total = parts * rows
    blocks = cols // LANES
    segs = rows // SEG
    local = min(cols, filters) // LANES
    owners = math.gcd(parts, local)
    per = local // owners
    kinds = filters // LANES // local
    reps = blocks // local
    scale = float(total) ** (-0.5)
    norm = float(total * cols * groups_chan // filters) ** (-0.5)
    whole = pl.BlockSpec(memory_space=pltpu.VMEM)
    far = pl.BlockSpec(memory_space=pl.ANY)
    shape = jax.ShapeDtypeStruct
    tiles = pltpu.VMEM((blocks, segs * PITCH, LANES), f32)
    states = pltpu.VMEM((blocks, segs * modes, LANES), f32)
    phases = pltpu.VMEM((reps, segs // PACK, SEG * PACK, LANES), bf16)
    dma = pltpu.SemaphoreType.DMA
    narrow = shape((rows, cols), bf16)
    near = pltpu.VMEM((rows, cols), bf16)
    results = pl.pallas_call(
        functools.partial(whole_kernel, scale, norm, parts, groups_chan, owners),
        out_shape=(near, near, near, pltpu.VMEM((2, modes, filters), f32)),
        in_specs=[pl.BlockSpec(memory_space=pltpu.HBM)] * 6,
        out_specs=(whole,) * 4,
        scratch_shapes=[
            pltpu.VMEM((4, blocks, rows, LANES), bf16),
            pltpu.VMEM((2, modes, filters), f32),
            tiles,
            tiles,
            tiles,
            tiles,
            states,
            states,
            pltpu.VMEM((parts, local, 4 * reps + 2, modes, LANES), bf16),
            pltpu.VMEM((2, modes, LANES), f32),
            pltpu.VMEM((local, SEG, LANES), f32),
            phases,
            phases,
            pltpu.VMEM((modes, LANES), f32),
            pltpu.VMEM(((SEG + 1) * modes, LANES), f32),
            pltpu.VMEM(((SEG + 1) * modes, LANES), f32),
            pltpu.VMEM((reps, 4, segs, LANES), f32),
            pltpu.VMEM((reps, 4, modes * (segs + 1), LANES), f32),
            pltpu.VMEM((SEG * SUB, LANES), f32),
            pltpu.VMEM((segs * (modes + 1), LANES), f32),
            pltpu.VMEM((segs * (modes + 1), LANES), f32),
            pltpu.VMEM((groups_chan, per, 2, modes, LANES), bf16),
            pltpu.VMEM((owners, kinds, per, 2, modes, LANES), bf16),
            dma((4, blocks)),
            dma((2,)),
            dma((parts, local)),
            dma((parts, local)),
            dma((groups_chan,)),
            dma((groups_chan,)),
            dma((owners,)),
            dma((owners,)),
        ],
        compiler_params=pltpu.CompilerParams(
            collective_id=0, has_side_effects=True
        ),
        name="whole",
    )(signal_in, gate_in, outer_gate, cotangent, residues, log_rates)
    results = [pltpu.with_memory_space_constraint(a, pltpu.VMEM) for a in results]
    return pl.pallas_call(
        pass_kernel,
        out_shape=(narrow, narrow, narrow, shape((modes, filters), f32), shape((modes, filters), f32)),
        in_specs=[whole] * 4,
        out_specs=(far,) * 5,
        scratch_shapes=[dma((5,))],
        name="passed",
    )(*results)


def solution(mesh):
    placed = (P("seq", "chan"), P("seq", "chan"), P("seq", "chan"), P("seq", "chan"), P(), P())
    return jax.shard_map(
        on_device,
        mesh=mesh,
        in_specs=placed,
        out_specs=(P("seq", "chan"), P("seq", "chan"), P("seq", "chan"), P(), P()),
        check_vma=False,
    )
```
